32 devices in a mesh: tm: 4 (over z), space: 8 (over y, x, core).
Axes of the slice: x: 2, y: 2, z: 4, core: 2. Of those that a mesh axis runs over, the one named last changes fastest.
Arguments:
- snapshots: bfloat16 [512, 393216], P('tm', 'space'), may hold values from -10 to 10, as said below
- area_weight: float32 [393216], P('space'), may hold values from 0.1 to 1
- eigvecs: bfloat16 [512, 64], replicated, may hold values from -0.25 to 0.25
- eigvals: float32 [64], replicated, may hold values from 0.5 to 8
Outputs:
- gram: float32 [512, 512], P(('tm', 'space'))
- modes: bfloat16 [64, 393216], P('tm', 'space')
The draws below stay inside these ranges and needn't reach their ends.
Inputs may be any that keep to these rules, and one draw needn't show every extreme that they name: `snapshots`: a per-column climatology plus hourly departures.
All inputs are finite; a program needn't handle non-finite values.
Results may differ from the reference program's by a relative error of at most 0.01.
Values may be sent and summed in bfloat16 or wider, within the bound.
No kernel may reach another device: no remote copies, remote signals or barrier semaphores. Data moves between devices by JAX's collectives and lax.ppermute only.
A program may use at most 128 MiB of HBM per device.

```python
import math
import jax
import jax.numpy as jnp
from jax import lax

CELL_DEV = 49152
MODES = 64
TIME = 512
CELLS = 393216


def draw_snapshots(key, part):
    first = jax.random.fold_in(key, 11)
    second = jax.random.fold_in(key, 12)
    climate = jax.random.uniform(first, (1, CELLS), jnp.float32, -2.0, 2.0)
    noise = jax.random.normal(second, (TIME, CELLS), jnp.float32)
    noise = jnp.clip(noise, -8.0, 8.0)
    return (climate + noise).astype(jnp.bfloat16)


def level_of(own_key, dims, split, low, top_value):
    factor_of, own = 1.0, jax.random.fold_in(own_key, 6)
    for dim, parts in split:
        steps = jnp.exp(jax.random.uniform(jax.random.fold_in(own, dim), (parts,), jnp.float32, low / len(split), top_value / len(split)))
        factor_of = factor_of * jnp.repeat(steps, dims[dim] // parts).reshape([-1 if axis == dim else 1 for axis in range(len(dims))])
    return factor_of


def centred(own_key, dims, deviation, reach, kind=jnp.bfloat16):
    return jnp.clip(deviation * jax.random.normal(own_key, dims, jnp.float32), -reach, reach).astype(kind)


def setup_inputs(seed: int = 0) -> dict:
    splits = jax.random.split(jax.random.key(seed), 5)
    return {
        "snapshots": draw_snapshots(jax.random.fold_in(splits[4], 71), 0),
        "area_weight": jnp.clip(jnp.exp(math.log(1.0) - 2.3025851 * jax.random.uniform(splits[1], (CELLS,), jnp.float32) ** level_of(splits[1], (CELLS,), ((0, 8),), -0.2, 0.2)), 0.1, 1.0),
        "eigvecs": centred(splits[2], (TIME, MODES), TIME ** -0.5, 0.25),
        "eigvals": jnp.clip(jnp.exp(jax.random.uniform(splits[3], (MODES,), jnp.float32, math.log(0.5), math.log(8.0))), 0.5, 8.0),
    }


def reference(snapshots, area_weight, eigvecs, eigvals):
    width = CELL_DEV
    count = CELLS // width
    inv_root = 1.0 / jnp.sqrt(eigvals)

    def step(total, index):
        start = (index * width).astype(jnp.int32)
        block = lax.dynamic_slice_in_dim(snapshots, start, width, 1).astype(jnp.float32)
        weight = lax.dynamic_slice_in_dim(area_weight, start, width, 0)
        mean = lax.optimization_barrier(jnp.sum(block, axis=0)) / TIME
        weighted = (jnp.sqrt(weight)[None, :] * (block - mean[None, :])).astype(jnp.bfloat16)
        part = lax.dot_general(weighted, weighted, (((1,), (1,)), ((), ())), preferred_element_type=jnp.float32)
        proj = jnp.dot(eigvecs.T, weighted, preferred_element_type=jnp.float32)
        mode_block = (proj * inv_root[:, None]).astype(jnp.bfloat16)
        return (total + part, mode_block)
    init = jnp.zeros((TIME, TIME), jnp.float32)
    total, mode_blocks = lax.scan(step, init, jnp.arange(count, dtype=jnp.int32))
    modes = jnp.transpose(mode_blocks, (1, 0, 2)).reshape(MODES, CELLS)
    return (total / CELLS, modes)
```

```python
import functools
import jax
import jax.numpy as jnp
from jax import lax
from jax.experimental import pallas as pl
from jax.experimental.pallas import tpu as pltpu
from jax.sharding import PartitionSpec as P

SHARES = (2, 8, 2)


def partner_table(count):
    if count & (count - 1) == 0:
        return lambda i, s: i ^ s, lambda i, s: i ^ s
    return lambda i, s: (i + s) % count, lambda i, s: (i - s) % count


def chunk_tiles(total):
    whole = sum(SHARES)
    ends = [round(total * sum(SHARES[: n + 1]) / whole) for n in range(len(SHARES))]
    starts = [0] + ends[:-1]
    return [(a, b) for a, b in zip(starts, ends) if b > a]


def chunk_kernel(times, time_dev, count, first, last, scale, source, where_ref, own_ref, *refs):
    recv_refs, refs = refs[: count - 1], refs[count - 1 :]
    root_ref, eig_ref, inv_ref = refs[:3]
    refs = refs[3:]
    if not first:
        prev_ref, refs = refs[0], refs[1:]
    mode_refs, refs = refs[:count], refs[count:]
    gram_ref, refs = refs[0], refs[1:]
    weighted, refs = refs[0], refs[1:]
    total = refs[0] if last else gram_ref
    step = pl.program_id(0)
    me = where_ref[0]
    width = own_ref.shape[1]
    rows = 16

    @pl.when(step == 0)
    def _():
        total[...] = jnp.zeros_like(total) if first else prev_ref[...]

    blocks = (own_ref,) + tuple(recv_refs)
    sums = jnp.zeros((rows, width), jnp.float32)
    for block in blocks:
        for r in range(0, time_dev, rows):
            sums = sums + block[r : r + rows, :].astype(jnp.float32)
    mean = jnp.sum(sums, axis=0, keepdims=True) / times
    root = root_ref[...]
    for s, block in enumerate(blocks):
        base = source(me, s) * time_dev
        for r in range(0, time_dev, rows):
            centred = block[r : r + rows, :].astype(jnp.float32) - mean
            weighted[pl.ds(pl.multiple_of(base + r, rows), rows), :] = (root * centred).astype(
                jnp.bfloat16
            )
    values = weighted[...]
    total[...] += lax.dot_general(
        values, values, (((1,), (1,)), ((), ())), preferred_element_type=jnp.float32
    )
    projected = jnp.dot(eig_ref[...], values, preferred_element_type=jnp.float32) * inv_ref[...]
    depth = mode_refs[0].shape[0]
    for s, mode_ref in enumerate(mode_refs):
        mode_ref[...] = projected[s * depth : (s + 1) * depth, :].astype(jnp.bfloat16)

    if last:

        @pl.when(step == pl.num_programs(0) - 1)
        def _():
            space_count, _, _ = gram_ref.shape
            block_rows = times // (space_count * count)
            for s in range(space_count):
                pieces = [
                    total[pl.ds((i * space_count + s) * block_rows, block_rows), :]
                    for i in range(count)
                ]
                gram_ref[s] = (jnp.concatenate(pieces, axis=0) * scale).astype(jnp.bfloat16)


def run_chunk(snapshots, recv, root, eig, inv, prev, where, lo, hi, tile, last, space_count, source):
    time_dev = snapshots.shape[0]
    count = len(recv) + 1
    times = time_dev * count
    steps = hi - lo
    depth = eig.shape[0] // count
    first = prev is None
    cells = snapshots.shape[1] * space_count
    kernel = functools.partial(
        chunk_kernel, times, time_dev, count, first, last, 1.0 / cells, source
    )
    in_specs = [pl.BlockSpec((time_dev, tile), lambda g, w: (0, w[1] + lo + g))]
    in_specs += [pl.BlockSpec((time_dev, tile), lambda g, w: (0, g))] * (count - 1)
    in_specs += [
        pl.BlockSpec((1, tile), lambda g, w: (0, lo + g)),
        pl.BlockSpec(eig.shape, lambda g, w: (0, 0)),
        pl.BlockSpec(inv.shape, lambda g, w: (0, 0)),
    ]
    operands = [snapshots, *recv, root, eig, inv]
    if not first:
        in_specs.append(pl.BlockSpec((times, times), lambda g, w: (0, 0)))
        operands.append(prev)
    out_specs = [pl.BlockSpec((depth, tile), lambda g, w: (0, g))] * count
    out_shape = [jax.ShapeDtypeStruct((depth, steps * tile), jnp.bfloat16)] * count
    scratch = [pltpu.VMEM((times, tile), jnp.bfloat16)]
    if last:
        shape = (space_count, times // space_count, times)
        out_specs.append(pl.BlockSpec(shape, lambda g, w: (0, 0, 0)))
        out_shape.append(jax.ShapeDtypeStruct(shape, jnp.bfloat16))
        scratch.append(pltpu.VMEM((times, times), jnp.float32))
    else:
        out_specs.append(pl.BlockSpec((times, times), lambda g, w: (0, 0)))
        out_shape.append(jax.ShapeDtypeStruct((times, times), jnp.float32))
    columns = steps * tile
    cost = pl.CostEstimate(
        flops=2 * times * (times + eig.shape[0]) * columns,
        bytes_accessed=2 * times * columns + 8 * times * times,
        transcendentals=0,
    )
    out = pl.pallas_call(
        kernel,
        out_shape=out_shape,
        grid_spec=pltpu.PrefetchScalarGridSpec(
            num_scalar_prefetch=1,
            grid=(steps,),
            in_specs=in_specs,
            out_specs=out_specs,
            scratch_shapes=scratch,
        ),
        cost_estimate=cost,
        name="chunk_last" if last else "chunk",
    )(where, *operands)
    return out[:count], out[count]


def local(snapshots, area_weight, eigvecs, eigvals):
    count = lax.axis_size("tm")
    space_count = lax.axis_size("space")
    me = lax.axis_index("tm")
    time_dev, cell_dev = snapshots.shape
    sub = cell_dev // count
    depth = eigvals.shape[0] // count
    tile = next(t for t in (1024, 512, 256, 128) if sub % t == 0)
    tiles = sub // tile
    chunks = chunk_tiles(tiles)
    target, source = partner_table(count)

    def permute(piece, s):
        return lax.ppermute(piece, "tm", [(i, target(i, s)) for i in range(count)])

    received = []
    for lo, hi in chunks:
        pieces = []
        for s in range(1, count):
            start = target(me, s) * sub + lo * tile
            piece = lax.dynamic_slice_in_dim(snapshots, start, (hi - lo) * tile, 1)
            pieces.append(permute(piece, s))
        received.append(pieces)

    own_weight = lax.dynamic_slice_in_dim(area_weight, me * sub, sub, 0)
    root = jnp.sqrt(own_weight)[None, :]
    eig_rows = eigvecs.T
    inv_rows = (1.0 / jnp.sqrt(eigvals))[:, None]
    order = [target(me, s) * depth for s in range(count)]
    eig = jnp.concatenate([lax.dynamic_slice_in_dim(eig_rows, o, depth, 0) for o in order], axis=0)
    inv = jnp.concatenate([lax.dynamic_slice_in_dim(inv_rows, o, depth, 0) for o in order], axis=0)
    where = jnp.stack([me, me * tiles]).astype(jnp.int32)

    gram = None
    mode_pieces = []
    for n, (lo, hi) in enumerate(chunks):
        last = n == len(chunks) - 1
        pieces, gram = run_chunk(
            snapshots, received[n], root, eig, inv, gram, where, lo, hi, tile, last, space_count, source
        )
        mode_pieces.append(pieces)

    rows = times_rows = gram.shape[1] // count
    parts = lax.all_to_all(gram, "space", split_axis=0, concat_axis=0, tiled=True)
    row_sums = jnp.sum(parts.astype(jnp.float32), axis=0).astype(jnp.bfloat16)
    row_sums = row_sums.reshape(count, rows, gram.shape[2])
    parts = lax.all_to_all(row_sums, "tm", split_axis=0, concat_axis=0, tiled=True)
    gram_rows = jnp.sum(parts.astype(jnp.float32), axis=0)

    modes = jnp.zeros((depth, cell_dev), jnp.bfloat16)
    for (lo, hi), pieces in zip(chunks, mode_pieces):
        for s, piece in enumerate(pieces):
            if s > 0:
                piece = permute(piece, s)
            modes = lax.dynamic_update_slice_in_dim(
                modes, piece, source(me, s) * sub + lo * tile, 1
            )
    return gram_rows, modes


def solution(mesh):
    in_specs = (P("tm", "space"), P("space"), P(), P())
    out_specs = (P(("tm", "space"), None), P("tm", "space"))
    return jax.shard_map(local, mesh=mesh, in_specs=in_specs, out_specs=out_specs, check_vma=False)
```

```python
import functools
import jax
import jax.numpy as jnp
from jax import lax
from jax.experimental import pallas as pl
from jax.experimental.pallas import tpu as pltpu
from jax.sharding import PartitionSpec as P

SHARES = (1, 8, 2, 1)
GROUPS = (0, 0, 1, 1)


def partner_table(count):
    if count & (count - 1) == 0:
        return lambda i, s: i ^ s, lambda i, s: i ^ s
    return lambda i, s: (i + s) % count, lambda i, s: (i - s) % count


def chunk_tiles(total):
    whole = sum(SHARES)
    ends = [round(total * sum(SHARES[: n + 1]) / whole) for n in range(len(SHARES))]
    starts = [0] + ends[:-1]
    return [(a, b, g) for a, b, g in zip(starts, ends, GROUPS) if b > a]


def tile_of(sub):
    return next((t for t in (1024, 512, 256) if sub % t == 0 and sub // t >= sum(SHARES)), 128)


def chunk_kernel(
    times, time_dev, count, first, last, carried, scale, source, where_ref, own_ref, *refs
):
    recv_refs, refs = refs[: count - 1], refs[count - 1 :]
    root_ref, eig_ref, inv_ref = refs[:3]
    refs = refs[3:]
    if not first:
        prev_ref, refs = refs[0], refs[1:]
    refs = refs[carried:]
    mode_refs, refs = refs[:count], refs[count:]
    gram_ref, refs = refs[0], refs[1:]
    weighted, refs = refs[0], refs[1:]
    total = refs[0] if last else gram_ref
    step = pl.program_id(0)
    me = where_ref[0]
    width = own_ref.shape[1]
    rows = 16

    @pl.when(step == 0)
    def _():
        total[...] = jnp.zeros_like(total) if first else prev_ref[...]

    blocks = (own_ref,) + tuple(recv_refs)
    sums = jnp.zeros((rows, width), jnp.float32)
    for block in blocks:
        for r in range(0, time_dev, rows):
            sums = sums + block[r : r + rows, :].astype(jnp.float32)
    mean = jnp.sum(sums, axis=0, keepdims=True) / times
    root = root_ref[...]
    for s, block in enumerate(blocks):
        base = source(me, s) * time_dev
        for r in range(0, time_dev, rows):
            centred = block[r : r + rows, :].astype(jnp.float32) - mean
            weighted[pl.ds(pl.multiple_of(base + r, rows), rows), :] = (root * centred).astype(
                jnp.bfloat16
            )
    values = weighted[...]
    total[...] += lax.dot_general(
        values, values, (((1,), (1,)), ((), ())), preferred_element_type=jnp.float32
    )
    projected = jnp.dot(eig_ref[...], values, preferred_element_type=jnp.float32) * inv_ref[...]
    depth = mode_refs[0].shape[0]
    for s, mode_ref in enumerate(mode_refs):
        mode_ref[...] = projected[s * depth : (s + 1) * depth, :].astype(jnp.bfloat16)

    if last:

        @pl.when(step == pl.num_programs(0) - 1)
        def _():
            space_count, _, _ = gram_ref.shape
            block_rows = times // (space_count * count)
            for s in range(space_count):
                pieces = [
                    total[pl.ds((i * space_count + s) * block_rows, block_rows), :]
                    for i in range(count)
                ]
                gram_ref[s] = (jnp.concatenate(pieces, axis=0) * scale).astype(jnp.bfloat16)


def run_chunk(
    snapshots, recv, root, eig, inv, prev, modes, where, span, group, tile, last, space_count, source
):
    lo, hi = span
    group_lo, group_hi = group
    time_dev = snapshots.shape[0]
    count = len(recv) + 1
    times = time_dev * count
    steps = hi - lo
    depth = eig.shape[0] // count
    first = prev is None
    cells = snapshots.shape[1] * space_count
    kernel = functools.partial(
        chunk_kernel, times, time_dev, count, first, last, len(modes), 1.0 / cells, source
    )
    in_specs = [pl.BlockSpec((time_dev, tile), lambda g, w: (0, w[1] + lo + g))]
    in_specs += [pl.BlockSpec((time_dev, tile), lambda g, w: (0, g))] * (count - 1)
    in_specs += [
        pl.BlockSpec((1, tile), lambda g, w: (0, lo + g)),
        pl.BlockSpec(eig.shape, lambda g, w: (0, 0)),
        pl.BlockSpec(inv.shape, lambda g, w: (0, 0)),
    ]
    operands = [snapshots, *recv, root, eig, inv]
    if not first:
        in_specs.append(pl.BlockSpec((times, times), lambda g, w: (0, 0)))
        operands.append(prev)
    aliases = {len(operands) + 1 + n: n for n in range(len(modes))}
    in_specs += [pl.BlockSpec(memory_space=pl.ANY)] * len(modes)
    operands += modes
    out_specs = [pl.BlockSpec((depth, tile), lambda g, w: (0, lo - group_lo + g))] * count
    out_shape = [jax.ShapeDtypeStruct((depth, (group_hi - group_lo) * tile), jnp.bfloat16)] * count
    scratch = [pltpu.VMEM((times, tile), jnp.bfloat16)]
    if last:
        shape = (space_count, times // space_count, times)
        out_specs.append(pl.BlockSpec(shape, lambda g, w: (0, 0, 0)))
        out_shape.append(jax.ShapeDtypeStruct(shape, jnp.bfloat16))
        scratch.append(pltpu.VMEM((times, times), jnp.float32))
    else:
        out_specs.append(pl.BlockSpec((times, times), lambda g, w: (0, 0)))
        out_shape.append(jax.ShapeDtypeStruct((times, times), jnp.float32))
    columns = steps * tile
    cost = pl.CostEstimate(
        flops=2 * times * (times + eig.shape[0]) * columns,
        bytes_accessed=2 * times * columns + 8 * times * times,
        transcendentals=0,
    )
    out = pl.pallas_call(
        kernel,
        out_shape=out_shape,
        grid_spec=pltpu.PrefetchScalarGridSpec(
            num_scalar_prefetch=1,
            grid=(steps,),
            in_specs=in_specs,
            out_specs=out_specs,
            scratch_shapes=scratch,
        ),
        input_output_aliases=aliases,
        cost_estimate=cost,
        name="chunk_last" if last else "chunk",
    )(where, *operands)
    return out[:count], out[count]


def local(snapshots, area_weight, eigvecs, eigvals):
    count = lax.axis_size("tm")
    space_count = lax.axis_size("space")
    me = lax.axis_index("tm")
    _, cell_dev = snapshots.shape
    sub = cell_dev // count
    depth = eigvals.shape[0] // count
    tile = tile_of(sub)
    tiles = sub // tile
    chunks = chunk_tiles(tiles)
    target, source = partner_table(count)

    def permute(piece, s):
        return lax.ppermute(piece, "tm", [(i, target(i, s)) for i in range(count)])

    received = []
    for lo, hi, _ in chunks:
        pieces = []
        for s in range(1, count):
            start = target(me, s) * sub + lo * tile
            piece = lax.dynamic_slice_in_dim(snapshots, start, (hi - lo) * tile, 1)
            pieces.append(permute(piece, s))
        received.append(pieces)

    own_weight = lax.dynamic_slice_in_dim(area_weight, me * sub, sub, 0)
    root = jnp.sqrt(own_weight)[None, :]
    eig_rows = eigvecs.T
    inv_rows = (1.0 / jnp.sqrt(eigvals))[:, None]
    order = [target(me, s) * depth for s in range(count)]
    eig = jnp.concatenate([lax.dynamic_slice_in_dim(eig_rows, o, depth, 0) for o in order], axis=0)
    inv = jnp.concatenate([lax.dynamic_slice_in_dim(inv_rows, o, depth, 0) for o in order], axis=0)
    where = jnp.stack([me, me * tiles]).astype(jnp.int32)

    gram = None
    groups = {}
    for n, (lo, hi, group) in enumerate(chunks):
        last = n == len(chunks) - 1
        members = [c for c in chunks if c[2] == group]
        bounds = (members[0][0], members[-1][1])
        pieces = groups[group][1] if group in groups else []
        pieces, gram = run_chunk(
            snapshots, received[n], root, eig, inv, gram, pieces, where,
            (lo, hi), bounds, tile, last, space_count, source,
        )
        groups[group] = (bounds[0], pieces)

    rows = gram.shape[1] // count
    parts = lax.all_to_all(gram, "space", split_axis=0, concat_axis=0, tiled=True)
    row_sums = jnp.sum(parts.astype(jnp.float32), axis=0).astype(jnp.bfloat16)
    row_sums = row_sums.reshape(count, rows, gram.shape[2])
    parts = lax.all_to_all(row_sums, "tm", split_axis=0, concat_axis=0, tiled=True)
    gram_rows = jnp.sum(parts.astype(jnp.float32), axis=0)

    modes = jnp.zeros((depth, cell_dev), jnp.bfloat16)
    modes, _ = lax.optimization_barrier((modes, row_sums))
    for (lo, pieces) in groups.values():
        for s, piece in enumerate(pieces):
            if s > 0:
                piece = permute(piece, s)
            modes = lax.dynamic_update_slice_in_dim(
                modes, piece, source(me, s) * sub + lo * tile, 1
            )
    return gram_rows, modes


def solution(mesh):
    in_specs = (P("tm", "space"), P("space"), P(), P())
    out_specs = (P(("tm", "space"), None), P("tm", "space"))

    return jax.shard_map(local, mesh=mesh, in_specs=in_specs, out_specs=out_specs, check_vma=False)
```

```python
import functools
import jax
import jax.numpy as jnp
from jax import lax
from jax.experimental import pallas as pl
from jax.experimental.pallas import tpu as pltpu
from jax.sharding import PartitionSpec as P

SHARES = (1, 8, 2, 1)
GROUPS = (0, 0, 1, 1)


def partner_table(count):
    if count & (count - 1) == 0:
        return lambda i, s: i ^ s, lambda i, s: i ^ s
    return lambda i, s: (i + s) % count, lambda i, s: (i - s) % count


def chunk_tiles(total):
    whole = sum(SHARES)
    ends = [round(total * sum(SHARES[: n + 1]) / whole) for n in range(len(SHARES))]
    starts = [0] + ends[:-1]
    return [(a, b, g) for a, b, g in zip(starts, ends, GROUPS) if b > a]


def tile_of(sub):
    return next((t for t in (1024, 512, 256) if sub % t == 0 and sub // t >= sum(SHARES)), 128)


def chunk_kernel(
    times, time_dev, count, first, last, carried, scale, source, where_ref, own_ref, *refs
):
    recv_refs, refs = refs[: count - 1], refs[count - 1 :]
    root_ref, eig_ref, inv_ref = refs[:3]
    refs = refs[3:]
    if not first:
        prev_ref, refs = refs[0], refs[1:]
    refs = refs[carried:]
    mode_refs, refs = refs[:count], refs[count:]
    gram_ref, refs = refs[0], refs[1:]
    weighted, refs = refs[0], refs[1:]
    total = refs[0] if last else gram_ref
    step = pl.program_id(0)
    me = where_ref[0]
    width = own_ref.shape[1]
    rows = 16

    @pl.when(step == 0)
    def _():
        total[...] = jnp.zeros_like(total) if first else prev_ref[...]

    blocks = (own_ref,) + tuple(recv_refs)
    sums = jnp.zeros((rows, width), jnp.float32)
    for block in blocks:
        for r in range(0, time_dev, rows):
            sums = sums + block[r : r + rows, :].astype(jnp.float32)
    mean = jnp.sum(sums, axis=0, keepdims=True) / times
    root = root_ref[...]
    for s, block in enumerate(blocks):
        base = source(me, s) * time_dev
        for r in range(0, time_dev, rows):
            centred = block[r : r + rows, :].astype(jnp.float32) - mean
            weighted[pl.ds(pl.multiple_of(base + r, rows), rows), :] = (root * centred).astype(
                jnp.bfloat16
            )
    values = weighted[...]
    total[...] += lax.dot_general(
        values, values, (((1,), (1,)), ((), ())), preferred_element_type=jnp.float32
    )
    projected = jnp.dot(eig_ref[...], values, preferred_element_type=jnp.float32) * inv_ref[...]
    depth = mode_refs[0].shape[0]
    for s, mode_ref in enumerate(mode_refs):
        mode_ref[...] = projected[s * depth : (s + 1) * depth, :].astype(jnp.bfloat16)

    if last:

        @pl.when(step == pl.num_programs(0) - 1)
        def _():
            space_count, _, _ = gram_ref.shape
            block_rows = times // (space_count * count)
            for s in range(space_count):
                pieces = [
                    total[pl.ds((i * space_count + s) * block_rows, block_rows), :]
                    for i in range(count)
                ]
                gram_ref[s] = (jnp.concatenate(pieces, axis=0) * scale).astype(jnp.bfloat16)


def run_chunk(
    snapshots, recv, root, eig, inv, prev, modes, where, span, group, tile, last, space_count, source
):
    lo, hi = span
    group_lo, group_hi = group
    time_dev = snapshots.shape[0]
    count = len(recv) + 1
    times = time_dev * count
    steps = hi - lo
    depth = eig.shape[0] // count
    first = prev is None
    cells = snapshots.shape[1] * space_count
    kernel = functools.partial(
        chunk_kernel, times, time_dev, count, first, last, len(modes), 1.0 / cells, source
    )
    in_specs = [pl.BlockSpec((time_dev, tile), lambda g, w: (0, w[1] + lo + g))]
    in_specs += [pl.BlockSpec((time_dev, tile), lambda g, w: (0, g))] * (count - 1)
    in_specs += [
        pl.BlockSpec((1, tile), lambda g, w: (0, lo + g)),
        pl.BlockSpec(eig.shape, lambda g, w: (0, 0)),
        pl.BlockSpec(inv.shape, lambda g, w: (0, 0)),
    ]
    operands = [snapshots, *recv, root, eig, inv]
    if not first:
        in_specs.append(pl.BlockSpec((times, times), lambda g, w: (0, 0)))
        operands.append(prev)
    aliases = {len(operands) + 1 + n: n for n in range(len(modes))}
    in_specs += [pl.BlockSpec(memory_space=pl.ANY)] * len(modes)
    operands += modes
    out_specs = [pl.BlockSpec((depth, tile), lambda g, w: (0, lo - group_lo + g))] * count
    out_shape = [jax.ShapeDtypeStruct((depth, (group_hi - group_lo) * tile), jnp.bfloat16)] * count
    scratch = [pltpu.VMEM((times, tile), jnp.bfloat16)]
    if last:
        shape = (space_count, times // space_count, times)
        out_specs.append(pl.BlockSpec(shape, lambda g, w: (0, 0, 0)))
        out_shape.append(jax.ShapeDtypeStruct(shape, jnp.bfloat16))
        scratch.append(pltpu.VMEM((times, times), jnp.float32))
    else:
        out_specs.append(pl.BlockSpec((times, times), lambda g, w: (0, 0)))
        out_shape.append(jax.ShapeDtypeStruct((times, times), jnp.float32))
    columns = steps * tile
    cost = pl.CostEstimate(
        flops=2 * times * (times + eig.shape[0]) * columns,
        bytes_accessed=2 * times * columns + 8 * times * times,
        transcendentals=0,
    )
    out = pl.pallas_call(
        kernel,
        out_shape=out_shape,
        grid_spec=pltpu.PrefetchScalarGridSpec(
            num_scalar_prefetch=1,
            grid=(steps,),
            in_specs=in_specs,
            out_specs=out_specs,
            scratch_shapes=scratch,
        ),
        input_output_aliases=aliases,
        cost_estimate=cost,
        name="chunk_last" if last else "chunk",
    )(where, *operands)
    return out[:count], out[count]


def local(snapshots, area_weight, eigvecs, eigvals):
    count = lax.axis_size("tm")
    space_count = lax.axis_size("space")
    me = lax.axis_index("tm")
    _, cell_dev = snapshots.shape
    sub = cell_dev // count
    depth = eigvals.shape[0] // count
    tile = tile_of(sub)
    tiles = sub // tile
    chunks = chunk_tiles(tiles)
    target, source = partner_table(count)

    def permute(piece, s):
        return lax.ppermute(piece, "tm", [(i, target(i, s)) for i in range(count)])

    received = []
    base = snapshots
    for n, (lo, hi, _) in enumerate(chunks):
        pieces = {}
        for s in reversed(range(1, count)):
            start = target(me, s) * sub + lo * tile
            piece = lax.dynamic_slice_in_dim(base, start, (hi - lo) * tile, 1)
            if n == 0:
                base, piece = lax.optimization_barrier((base, piece))
            pieces[s] = permute(piece, s)
        received.append([pieces[s] for s in range(1, count)])

    own_weight = lax.dynamic_slice_in_dim(area_weight, me * sub, sub, 0)
    root = jnp.sqrt(own_weight)[None, :]
    eig_rows = eigvecs.T
    inv_rows = (1.0 / jnp.sqrt(eigvals))[:, None]
    order = [target(me, s) * depth for s in range(count)]
    eig = jnp.concatenate([lax.dynamic_slice_in_dim(eig_rows, o, depth, 0) for o in order], axis=0)
    inv = jnp.concatenate([lax.dynamic_slice_in_dim(inv_rows, o, depth, 0) for o in order], axis=0)
    where = jnp.stack([me, me * tiles]).astype(jnp.int32)

    gram = None
    groups = {}
    for n, (lo, hi, group) in enumerate(chunks):
        last = n == len(chunks) - 1
        members = [c for c in chunks if c[2] == group]
        bounds = (members[0][0], members[-1][1])
        pieces = groups[group][1] if group in groups else []
        pieces, gram = run_chunk(
            snapshots, received[n], root, eig, inv, gram, pieces, where,
            (lo, hi), bounds, tile, last, space_count, source,
        )
        groups[group] = (bounds[0], pieces)

    rows = gram.shape[1] // count
    parts = lax.all_to_all(gram, "space", split_axis=0, concat_axis=0, tiled=True)
    row_sums = jnp.sum(parts.astype(jnp.float32), axis=0).astype(jnp.bfloat16)
    row_sums = row_sums.reshape(count, rows, gram.shape[2])
    parts = lax.all_to_all(row_sums, "tm", split_axis=0, concat_axis=0, tiled=True)
    gram_rows = jnp.sum(parts.astype(jnp.float32), axis=0)

    modes = jnp.zeros((depth, cell_dev), jnp.bfloat16)
    modes, _ = lax.optimization_barrier((modes, row_sums))
    for (lo, pieces) in groups.values():
        for s, piece in enumerate(pieces):
            if s > 0:
                piece = permute(piece, s)
            modes = lax.dynamic_update_slice_in_dim(
                modes, piece, source(me, s) * sub + lo * tile, 1
            )
    return gram_rows, modes


def solution(mesh):
    in_specs = (P("tm", "space"), P("space"), P(), P())
    out_specs = (P(("tm", "space"), None), P("tm", "space"))

    return jax.shard_map(local, mesh=mesh, in_specs=in_specs, out_specs=out_specs, check_vma=False)
```

```python
import functools
import jax
import jax.numpy as jnp
from jax import lax
from jax.experimental import pallas as pl
from jax.experimental.pallas import tpu as pltpu
from jax.sharding import PartitionSpec as P

SHARES = (1, 8, 2, 1)
GROUPS = (0, 0, 1, 1)


def partner_table(count):
    if count & (count - 1) == 0:
        return lambda i, s: i ^ s, lambda i, s: i ^ s
    return lambda i, s: (i + s) % count, lambda i, s: (i - s) % count


def chunk_tiles(total):
    whole = sum(SHARES)
    ends = [round(total * sum(SHARES[: n + 1]) / whole) for n in range(len(SHARES))]
    starts = [0] + ends[:-1]
    return [(a, b, g) for a, b, g in zip(starts, ends, GROUPS) if b > a]


def tile_of(sub):
    return next((t for t in (1024, 512, 256) if sub % t == 0 and sub // t >= sum(SHARES)), 128)


def chunk_kernel(
    times, time_dev, count, first, last, carried, scale, target, source, where_ref, own_ref, *refs
):
    recv_refs, refs = refs[: count - 1], refs[count - 1 :]
    root_ref, eig_ref, inv_ref = refs[:3]
    refs = refs[3:]
    if not first:
        prev_ref, refs = refs[0], refs[1:]
    refs = refs[carried:]
    mode_refs, refs = refs[:count], refs[count:]
    gram_ref, refs = refs[0], refs[1:]
    weighted, refs = refs[0], refs[1:]
    total = refs[0] if last else gram_ref
    step = pl.program_id(0)
    me = where_ref[0]
    width = own_ref.shape[1]
    rows = 16

    @pl.when(step == 0)
    def _():
        total[...] = jnp.zeros_like(total) if first else prev_ref[...]

    blocks = (own_ref,) + tuple(recv_refs)
    sums = jnp.zeros((rows, width), jnp.float32)
    for block in blocks:
        for r in range(0, time_dev, rows):
            sums = sums + block[r : r + rows, :].astype(jnp.float32)
    mean = jnp.sum(sums, axis=0, keepdims=True) / times
    root = root_ref[...]
    for s, block in enumerate(blocks):
        base = source(me, s) * time_dev
        for r in range(0, time_dev, rows):
            centred = block[r : r + rows, :].astype(jnp.float32) - mean
            weighted[pl.ds(pl.multiple_of(base + r, rows), rows), :] = (root * centred).astype(
                jnp.bfloat16
            )
    values = weighted[...]
    total[...] += lax.dot_general(
        values, values, (((1,), (1,)), ((), ())), preferred_element_type=jnp.float32
    )
    projected = jnp.dot(eig_ref[...], values, preferred_element_type=jnp.float32) * inv_ref[...]
    depth = mode_refs[0].shape[0]
    for s, mode_ref in enumerate(mode_refs):
        mode_ref[...] = projected[s * depth : (s + 1) * depth, :].astype(jnp.bfloat16)

    if last:

        @pl.when(step == pl.num_programs(0) - 1)
        def _():
            space_count, _, _ = gram_ref.shape
            block_rows = times // (space_count * count)
            for s in range(space_count):
                pieces = [
                    total[
                        pl.ds(
                            pl.multiple_of((target(me, i) * space_count + s) * block_rows, block_rows),
                            block_rows,
                        ),
                        :,
                    ]
                    for i in range(count)
                ]
                gram_ref[s] = (jnp.concatenate(pieces, axis=0) * scale).astype(jnp.bfloat16)


def run_chunk(
    snapshots, recv, root, eig, inv, prev, modes, where, span, group, tile, last, space_count, target, source
):
    lo, hi = span
    group_lo, group_hi = group
    time_dev = snapshots.shape[0]
    count = len(recv) + 1
    times = time_dev * count
    steps = hi - lo
    depth = eig.shape[0] // count
    first = prev is None
    cells = snapshots.shape[1] * space_count
    kernel = functools.partial(
        chunk_kernel, times, time_dev, count, first, last, len(modes), 1.0 / cells, target, source
    )
    in_specs = [pl.BlockSpec((time_dev, tile), lambda g, w: (0, w[1] + lo + g))]
    in_specs += [pl.BlockSpec((time_dev, tile), lambda g, w: (0, g))] * (count - 1)
    in_specs += [
        pl.BlockSpec((1, tile), lambda g, w: (0, lo + g)),
        pl.BlockSpec(eig.shape, lambda g, w: (0, 0)),
        pl.BlockSpec(inv.shape, lambda g, w: (0, 0)),
    ]
    operands = [snapshots, *recv, root, eig, inv]
    if not first:
        in_specs.append(pl.BlockSpec((times, times), lambda g, w: (0, 0)))
        operands.append(prev)
    aliases = {len(operands) + 1 + n: n for n in range(len(modes))}
    in_specs += [pl.BlockSpec(memory_space=pl.ANY)] * len(modes)
    operands += modes
    out_specs = [pl.BlockSpec((depth, tile), lambda g, w: (0, lo - group_lo + g))] * count
    out_shape = [jax.ShapeDtypeStruct((depth, (group_hi - group_lo) * tile), jnp.bfloat16)] * count
    scratch = [pltpu.VMEM((times, tile), jnp.bfloat16)]
    if last:
        shape = (space_count, times // space_count, times)
        out_specs.append(pl.BlockSpec(shape, lambda g, w: (0, 0, 0)))
        out_shape.append(jax.ShapeDtypeStruct(shape, jnp.bfloat16))
        scratch.append(pltpu.VMEM((times, times), jnp.float32))
    else:
        out_specs.append(pl.BlockSpec((times, times), lambda g, w: (0, 0)))
        out_shape.append(jax.ShapeDtypeStruct((times, times), jnp.float32))
    columns = steps * tile
    cost = pl.CostEstimate(
        flops=2 * times * (times + eig.shape[0]) * columns,
        bytes_accessed=2 * times * columns + 8 * times * times,
        transcendentals=0,
    )
    out = pl.pallas_call(
        kernel,
        out_shape=out_shape,
        grid_spec=pltpu.PrefetchScalarGridSpec(
            num_scalar_prefetch=1,
            grid=(steps,),
            in_specs=in_specs,
            out_specs=out_specs,
            scratch_shapes=scratch,
        ),
        input_output_aliases=aliases,
        cost_estimate=cost,
        name="chunk_last" if last else "chunk",
    )(where, *operands)
    return out[:count], out[count]


def local(snapshots, area_weight, eigvecs, eigvals):
    count = lax.axis_size("tm")
    space_count = lax.axis_size("space")
    me = lax.axis_index("tm")
    _, cell_dev = snapshots.shape
    sub = cell_dev // count
    depth = eigvals.shape[0] // count
    tile = tile_of(sub)
    tiles = sub // tile
    chunks = chunk_tiles(tiles)
    target, source = partner_table(count)

    def permute(piece, s):
        return lax.ppermute(piece, "tm", [(i, target(i, s)) for i in range(count)])

    received = []
    base = snapshots
    for n, (lo, hi, _) in enumerate(chunks):
        pieces = {}
        for s in reversed(range(1, count)):
            start = target(me, s) * sub + lo * tile
            piece = lax.dynamic_slice_in_dim(base, start, (hi - lo) * tile, 1)
            if n == 0:
                base, piece = lax.optimization_barrier((base, piece))
            pieces[s] = permute(piece, s)
        received.append([pieces[s] for s in range(1, count)])

    own_weight = lax.dynamic_slice_in_dim(area_weight, me * sub, sub, 0)
    root = jnp.sqrt(own_weight)[None, :]
    eig_rows = eigvecs.T
    inv_rows = (1.0 / jnp.sqrt(eigvals))[:, None]
    order = [target(me, s) * depth for s in range(count)]
    eig = jnp.concatenate([lax.dynamic_slice_in_dim(eig_rows, o, depth, 0) for o in order], axis=0)
    inv = jnp.concatenate([lax.dynamic_slice_in_dim(inv_rows, o, depth, 0) for o in order], axis=0)
    where = jnp.stack([me, me * tiles]).astype(jnp.int32)

    gram = None
    groups = {}
    for n, (lo, hi, group) in enumerate(chunks):
        last = n == len(chunks) - 1
        members = [c for c in chunks if c[2] == group]
        bounds = (members[0][0], members[-1][1])
        pieces = groups[group][1] if group in groups else []
        pieces, gram = run_chunk(
            snapshots, received[n], root, eig, inv, gram, pieces, where,
            (lo, hi), bounds, tile, last, space_count, target, source,
        )
        groups[group] = (bounds[0], pieces)

    rows = gram.shape[1] // count
    parts = lax.all_to_all(gram, "space", split_axis=0, concat_axis=0, tiled=True)
    row_sums = [
        jnp.sum(parts[:, s * rows : (s + 1) * rows].astype(jnp.float32), axis=0)
        for s in range(count)
    ]
    gram_rows = row_sums[0]
    for s in range(1, count):
        gram_rows = gram_rows + permute(row_sums[s].astype(jnp.bfloat16), s).astype(jnp.float32)

    modes = jnp.zeros((depth, cell_dev), jnp.bfloat16)
    modes, _ = lax.optimization_barrier((modes, row_sums[0]))
    for (lo, pieces) in groups.values():
        for s, piece in enumerate(pieces):
            if s > 0:
                piece = permute(piece, s)
            modes = lax.dynamic_update_slice_in_dim(
                modes, piece, source(me, s) * sub + lo * tile, 1
            )
    return gram_rows, modes


def solution(mesh):
    in_specs = (P("tm", "space"), P("space"), P(), P())
    out_specs = (P(("tm", "space"), None), P("tm", "space"))

    return jax.shard_map(local, mesh=mesh, in_specs=in_specs, out_specs=out_specs, check_vma=False)
```

```python
import functools
import jax
import jax.numpy as jnp
from jax import lax
from jax.experimental import pallas as pl
from jax.experimental.pallas import tpu as pltpu
from jax.sharding import PartitionSpec as P

SHARES = (1, 8, 2, 1)
GROUPS = (0, 0, 1, 1)


def partner_table(count):
    if count & (count - 1) == 0:
        return lambda i, s: i ^ s, lambda i, s: i ^ s
    return lambda i, s: (i + s) % count, lambda i, s: (i - s) % count


def chunk_tiles(total):
    whole = sum(SHARES)
    ends = [round(total * sum(SHARES[: n + 1]) / whole) for n in range(len(SHARES))]
    starts = [0] + ends[:-1]
    return [(a, b, g) for a, b, g in zip(starts, ends, GROUPS) if b > a]


def tile_of(sub):
    return next((t for t in (1024, 512, 256) if sub % t == 0 and sub // t >= sum(SHARES)), 128)


def chunk_kernel(
    times, time_dev, count, first, last, carried, scale, target, source, where_ref, own_ref, *refs
):
    recv_refs, refs = refs[: count - 1], refs[count - 1 :]
    root_ref, eig_ref, inv_ref = refs[:3]
    refs = refs[3:]
    if not first:
        prev_ref, refs = refs[0], refs[1:]
    refs = refs[carried:]
    mode_refs, refs = refs[:count], refs[count:]
    gram_ref, refs = refs[0], refs[1:]
    weighted, refs = refs[0], refs[1:]
    total = refs[0] if last else gram_ref
    step = pl.program_id(0)
    me = where_ref[0]
    width = own_ref.shape[1]
    rows = 16

    @pl.when(step == 0)
    def _():
        total[...] = jnp.zeros_like(total) if first else prev_ref[...]

    blocks = (own_ref,) + tuple(recv_refs)
    sums = jnp.zeros((rows, width), jnp.float32)
    for block in blocks:
        for r in range(0, time_dev, rows):
            sums = sums + block[r : r + rows, :].astype(jnp.float32)
    mean = jnp.sum(sums, axis=0, keepdims=True) / times
    root = root_ref[...]
    for s, block in enumerate(blocks):
        base = source(me, s) * time_dev
        for r in range(0, time_dev, rows):
            centred = block[r : r + rows, :].astype(jnp.float32) - mean
            weighted[pl.ds(pl.multiple_of(base + r, rows), rows), :] = (root * centred).astype(
                jnp.bfloat16
            )
    values = weighted[...]
    total[...] += lax.dot_general(
        values, values, (((1,), (1,)), ((), ())), preferred_element_type=jnp.float32
    )
    projected = jnp.dot(eig_ref[...], values, preferred_element_type=jnp.float32) * inv_ref[...]
    depth = mode_refs[0].shape[0]
    for s, mode_ref in enumerate(mode_refs):
        mode_ref[...] = projected[s * depth : (s + 1) * depth, :].astype(jnp.bfloat16)

    if last:

        @pl.when(step == pl.num_programs(0) - 1)
        def _():
            space_count, _, _ = gram_ref.shape
            block_rows = times // (space_count * count)
            for s in range(space_count):
                pieces = [
                    total[
                        pl.ds(
                            pl.multiple_of((target(me, i) * space_count + s) * block_rows, block_rows),
                            block_rows,
                        ),
                        :,
                    ]
                    for i in range(count)
                ]
                gram_ref[s] = (jnp.concatenate(pieces, axis=0) * scale).astype(jnp.bfloat16)


def run_chunk(
    snapshots, recv, root, eig, inv, prev, modes, where, span, group, tile, last, space_count, target, source
):
    lo, hi = span
    group_lo, group_hi = group
    time_dev = snapshots.shape[0]
    count = len(recv) + 1
    times = time_dev * count
    steps = hi - lo
    depth = eig.shape[0] // count
    first = prev is None
    cells = snapshots.shape[1] * space_count
    kernel = functools.partial(
        chunk_kernel, times, time_dev, count, first, last, len(modes), 1.0 / cells, target, source
    )
    in_specs = [pl.BlockSpec((time_dev, tile), lambda g, w: (0, w[1] + lo + g))]
    in_specs += [pl.BlockSpec((time_dev, tile), lambda g, w: (0, g))] * (count - 1)
    in_specs += [
        pl.BlockSpec((1, tile), lambda g, w: (0, lo + g)),
        pl.BlockSpec(eig.shape, lambda g, w: (0, 0)),
        pl.BlockSpec(inv.shape, lambda g, w: (0, 0)),
    ]
    operands = [snapshots, *recv, root, eig, inv]
    if not first:
        in_specs.append(pl.BlockSpec((times, times), lambda g, w: (0, 0)))
        operands.append(prev)
    aliases = {len(operands) + 1 + n: n for n in range(len(modes))}
    in_specs += [pl.BlockSpec(memory_space=pl.ANY)] * len(modes)
    operands += modes
    out_specs = [pl.BlockSpec((depth, tile), lambda g, w: (0, lo - group_lo + g))] * count
    out_shape = [jax.ShapeDtypeStruct((depth, (group_hi - group_lo) * tile), jnp.bfloat16)] * count
    scratch = [pltpu.VMEM((times, tile), jnp.bfloat16)]
    if last:
        shape = (space_count, times // space_count, times)
        out_specs.append(pl.BlockSpec(shape, lambda g, w: (0, 0, 0)))
        out_shape.append(jax.ShapeDtypeStruct(shape, jnp.bfloat16))
        scratch.append(pltpu.VMEM((times, times), jnp.float32))
    else:
        out_specs.append(pl.BlockSpec((times, times), lambda g, w: (0, 0)))
        out_shape.append(jax.ShapeDtypeStruct((times, times), jnp.float32))
    columns = steps * tile
    cost = pl.CostEstimate(
        flops=2 * times * (times + eig.shape[0]) * columns,
        bytes_accessed=2 * times * columns + 8 * times * times,
        transcendentals=0,
    )
    out = pl.pallas_call(
        kernel,
        out_shape=out_shape,
        grid_spec=pltpu.PrefetchScalarGridSpec(
            num_scalar_prefetch=1,
            grid=(steps,),
            in_specs=in_specs,
            out_specs=out_specs,
            scratch_shapes=scratch,
        ),
        input_output_aliases=aliases,
        cost_estimate=cost,
        name="chunk_last" if last else "chunk",
    )(where, *operands)
    return out[:count], out[count]


def local(snapshots, area_weight, eigvecs, eigvals):
    count = lax.axis_size("tm")
    space_count = lax.axis_size("space")
    me = lax.axis_index("tm")
    _, cell_dev = snapshots.shape
    sub = cell_dev // count
    depth = eigvals.shape[0] // count
    tile = tile_of(sub)
    tiles = sub // tile
    chunks = chunk_tiles(tiles)
    target, source = partner_table(count)

    def permute(piece, s):
        return lax.ppermute(piece, "tm", [(i, target(i, s)) for i in range(count)])

    received = []
    base = snapshots
    for lo, hi, _ in chunks:
        pieces = {}
        for s in reversed(range(1, count)):
            start = target(me, s) * sub + lo * tile
            piece = lax.dynamic_slice_in_dim(base, start, (hi - lo) * tile, 1)
            base, piece = lax.optimization_barrier((base, piece))
            pieces[s] = permute(piece, s)
        received.append([pieces[s] for s in range(1, count)])

    own_weight = lax.dynamic_slice_in_dim(area_weight, me * sub, sub, 0)
    root = jnp.sqrt(own_weight)[None, :]
    eig_rows = eigvecs.T
    inv_rows = (1.0 / jnp.sqrt(eigvals))[:, None]
    order = [target(me, s) * depth for s in range(count)]
    eig = jnp.concatenate([lax.dynamic_slice_in_dim(eig_rows, o, depth, 0) for o in order], axis=0)
    inv = jnp.concatenate([lax.dynamic_slice_in_dim(inv_rows, o, depth, 0) for o in order], axis=0)
    where = jnp.stack([me, me * tiles]).astype(jnp.int32)

    gram = None
    groups = {}
    for n, (lo, hi, group) in enumerate(chunks):
        last = n == len(chunks) - 1
        members = [c for c in chunks if c[2] == group]
        bounds = (members[0][0], members[-1][1])
        pieces = groups[group][1] if group in groups else []
        pieces, gram = run_chunk(
            snapshots, received[n], root, eig, inv, gram, pieces, where,
            (lo, hi), bounds, tile, last, space_count, target, source,
        )
        groups[group] = (bounds[0], pieces)

    rows = gram.shape[1] // count
    parts = lax.all_to_all(gram, "space", split_axis=0, concat_axis=0, tiled=True)
    held = {}
    for s in range(count):
        held[s] = jnp.sum(parts[:, s * rows : (s + 1) * rows].astype(jnp.float32), axis=0)
    row_sums = held[0]
    if count & (count - 1) == 0:
        bit = 1
        while bit < count:
            moved = [s for s in held if s & bit]
            packed = jnp.concatenate([held[s] for s in moved], axis=0).astype(jnp.bfloat16)
            packed = permute(packed, bit).astype(jnp.float32)
            for n, s in enumerate(moved):
                held[s ^ bit] = held[s ^ bit] + packed[n * rows : (n + 1) * rows]
                del held[s]
            bit *= 2
        gram_rows = held[0]
    else:
        gram_rows = held[0]
        for s in range(1, count):
            moved = permute(held[s].astype(jnp.bfloat16), s)
            gram_rows = gram_rows + moved.astype(jnp.float32)

    modes = jnp.zeros((depth, cell_dev), jnp.bfloat16)
    modes, _ = lax.optimization_barrier((modes, row_sums))
    for (lo, pieces) in groups.values():
        for s, piece in enumerate(pieces):
            if s > 0:
                piece = permute(piece, s)
            modes = lax.dynamic_update_slice_in_dim(
                modes, piece, source(me, s) * sub + lo * tile, 1
            )
    return gram_rows, modes


def solution(mesh):
    in_specs = (P("tm", "space"), P("space"), P(), P())
    out_specs = (P(("tm", "space"), None), P("tm", "space"))

    return jax.shard_map(local, mesh=mesh, in_specs=in_specs, out_specs=out_specs, check_vma=False)
```
